128 devices in a mesh: group: 32 (over z_lo, y, x), cls: 4 (over z_hi, core).
Axes of the slice: x: 4, y: 4, z: 4 (z_hi: 2, z_lo: 2; z = z_hi * 2 + z_lo), core: 2. Of those that a mesh axis runs over, the one named last changes fastest.
Arguments:
- features: bfloat16 [32768, 512], P(('group', 'cls')), may hold values from -6 to 6
- student_logits: bfloat16 [32768, 6656], P('group', 'cls'), may hold values from -100 to 320
- line_lengths: int32 [128], P(('group', 'cls')), may hold values from 64 to 256, as said below
- teacher_group: int32 [1], replicated, may hold values from 0 to 31
- pointwise_weight: bfloat16 [32, 512, 512], P('group'), may hold values from -0.25 to 0.25
- up_weight: bfloat16 [32, 512, 2048], P('group'), may hold values from -0.25 to 0.25
- down_weight: bfloat16 [32, 2048, 512], P('group'), may hold values from -0.125 to 0.125
- class_weight: bfloat16 [32, 512, 6656], P('group', None, 'cls'), may hold values from -9 to 9
- conv_kernel: bfloat16 [32, 3, 512], P('group'), may hold values from -3 to 3
- norm_gains: bfloat16 [32, 2, 512], P('group'), may hold values from 0.5 to 1.5
Outputs:
- divergence: float32 [32768], P(('group', 'cls'))
The draws below stay inside these ranges and needn't reach their ends.
Inputs may be any that keep to these rules, and one draw needn't show every extreme that they name: `line_lengths`: every line has at least 64 frames in use, and some line uses all 256.
All inputs are finite; a program needn't handle non-finite values.
Results may differ from the reference program's by a relative error of at most 0.035.
Values may be sent and summed in bfloat16 or wider, within the bound.
A program may use at most 64 MiB of HBM per device.

```python
import math
import jax
import jax.numpy as jnp
from jax import lax

D = 512
FF = 2048
V = 6656
FRAMES = 256
GROUPS = 32
FR_GRP = 1024
FR_ALL = 32768
LINES = 128


def draw_line_lengths(key, part):
    values = jax.random.randint(key, (LINES,), FRAMES // 4, FRAMES + 1)
    values = values.at[0].set(FRAMES)
    values = values.at[1].set(FRAMES // 4)
    return values.astype(jnp.int32)


def draw_student_logits(key, part):
    keys = jax.random.split(key, 3)
    row_scale = jnp.exp(jax.random.uniform(keys[1], (FR_ALL, 1), jnp.float32, 0.0, math.log(4.0)))
    col_scale = jnp.exp(jax.random.uniform(keys[2], (1, V), jnp.float32, 0.0, math.log(4.0)))
    base = jnp.clip(jax.random.normal(keys[0], (FR_ALL, V), jnp.float32), -6.0, 6.0)
    values = base * row_scale * col_scale
    return values.astype(jnp.bfloat16)


def draw_class_weight(key, part):
    keys = jax.random.split(key, 2)
    col_scale = 5.0 * jnp.exp(jax.random.uniform(keys[1], (GROUPS, 1, V), jnp.float32, 0.0, math.log(1.2)))
    base = jnp.clip(jax.random.normal(keys[0], (GROUPS, D, V), jnp.float32), -6.0, 6.0)
    values = base * col_scale * (0.8 / math.sqrt(D))
    return values.astype(jnp.bfloat16)


def steps_of(own_key, dims, cuts, least, top_value):
    level = 1.0
    for axis_at, shards_of in cuts:
        draws = jax.random.uniform(jax.random.fold_in(jax.random.fold_in(own_key, 6), axis_at), (shards_of,), jnp.float32, least / len(cuts), top_value / len(cuts))
        level = level * jnp.repeat(jnp.exp(draws), dims[axis_at] // shards_of).reshape((-1,) + (1,) * (len(dims) - 1 - axis_at))
    return level


def gaussian(stream_key, extent, spread, limit, cuts=(), kind=jnp.bfloat16):
    loudness = steps_of(stream_key, extent, cuts, -0.22, 0.18) if cuts else 1.0
    drawn = jax.random.normal(stream_key, extent, jnp.float32) * spread * loudness
    return jnp.minimum(jnp.maximum(drawn, -limit), limit).astype(kind)


def setup_inputs(seed: int = 0) -> dict:
    key_list = jax.random.split(jax.random.key(seed), 11)
    features = gaussian(key_list[0], (FR_ALL, D), 1.0, 6.0, ((0, 128),))
    student_logits = draw_student_logits(jax.random.fold_in(key_list[10], 71), 0)
    line_lengths = draw_line_lengths(jax.random.fold_in(key_list[10], 71), 0)
    teacher_group = jax.random.randint(key_list[3], (1,), 0, GROUPS).astype(jnp.int32)
    pointwise_weight = gaussian(key_list[4], (GROUPS, D, D), D ** -0.5, 0.25, ((0, 32),))
    up_weight = gaussian(key_list[5], (GROUPS, D, FF), D ** -0.5, 0.25, ((0, 32),))
    down_weight = gaussian(key_list[6], (GROUPS, FF, D), FF ** -0.5, 0.125, ((0, 32),))
    class_weight = draw_class_weight(jax.random.fold_in(key_list[10], 71), 0)
    conv_kernel = gaussian(key_list[8], (GROUPS, 3, D), 0.5, 3.0, ((0, 32),))
    norm_gains = jnp.clip(1.0 + 0.1 * jax.random.normal(key_list[9], (GROUPS, 2, D), jnp.float32), 0.5, 1.5).astype(jnp.bfloat16)
    return dict(features=features, student_logits=student_logits, line_lengths=line_lengths, teacher_group=teacher_group, pointwise_weight=pointwise_weight, up_weight=up_weight, down_weight=down_weight, class_weight=class_weight, conv_kernel=conv_kernel, norm_gains=norm_gains)


EPS = 1e-06

def frame_mask(line_lengths):
    positions = jnp.arange(FRAMES, dtype=jnp.int32)
    return (positions[None, :] < line_lengths[:, None]).astype(jnp.float32).reshape(-1)

def rms_scale(values, gain):
    return values * lax.rsqrt(lax.optimization_barrier(jnp.mean(values * values, axis=-1, keepdims=True)) + EPS) * gain.astype(jnp.float32)

def teacher_layer(features, line_lengths, pointwise, up_proj, down_proj, kernel, gain_first, gain_second):
    mask = frame_mask(line_lengths)
    inputs = features.astype(jnp.float32)
    masked = (inputs * mask[:, None]).reshape(-1, FRAMES, inputs.shape[1])
    padded = jnp.pad(masked, ((0, 0), (1, 1), (0, 0)))
    kern = kernel.astype(jnp.float32)
    conv = kern[0] * padded[:, :-2] + kern[1] * padded[:, 1:-1] + kern[2] * padded[:, 2:]
    conv = conv.reshape(inputs.shape).astype(jnp.bfloat16)
    resid = inputs + jnp.dot(conv, pointwise, preferred_element_type=jnp.float32)
    normed = rms_scale(resid, gain_first).astype(jnp.bfloat16)
    hidden = jax.nn.gelu(jnp.dot(normed, up_proj, preferred_element_type=jnp.float32)).astype(jnp.bfloat16)
    output = resid + jnp.dot(hidden, down_proj, preferred_element_type=jnp.float32)
    return (rms_scale(output, gain_second).astype(jnp.bfloat16), mask)

def row_kl(teacher_rows, student_rows):
    teach = teacher_rows.astype(jnp.float32)
    stud = student_rows.astype(jnp.float32)
    t_max = lax.optimization_barrier(jnp.max(teach, axis=-1, keepdims=True))
    t_exp = jnp.exp(teach - t_max)
    t_sum = lax.optimization_barrier(jnp.sum(t_exp, axis=-1))
    s_max = lax.optimization_barrier(jnp.max(stud, axis=-1, keepdims=True))
    s_sum = lax.optimization_barrier(jnp.sum(jnp.exp(stud - s_max), axis=-1))
    cross = lax.optimization_barrier(jnp.sum(t_exp * (teach - stud), axis=-1))
    return cross / t_sum - (t_max[:, 0] + jnp.log(t_sum)) + (s_max[:, 0] + jnp.log(s_sum))

def blocked_kl(teacher_logits, student_logits):
    rows = teacher_logits.shape[0]
    block = math.gcd(rows, 512)
    count = rows // block
    pairs = (teacher_logits.reshape(count, block, -1), student_logits.reshape(count, block, -1))
    return lax.map(lambda pair: row_kl(pair[0], pair[1]), pairs).reshape(rows)

def reference(features, student_logits, line_lengths, teacher_group, pointwise_weight, up_weight, down_weight, class_weight, conv_kernel, norm_gains):
    source = teacher_group[0]
    pointwise = pointwise_weight[source]
    up_proj = up_weight[source]
    down_proj = down_weight[source]
    classes = class_weight[source]
    kernel = conv_kernel[source]
    gains = norm_gains[source]

    def one_group(inputs):
        feats, lengths, students = inputs
        final, mask = teacher_layer(feats, lengths, pointwise, up_proj, down_proj, kernel, gains[0], gains[1])
        logits = jnp.dot(final, classes, preferred_element_type=jnp.float32).astype(jnp.bfloat16)
        return blocked_kl(logits, students) * mask
    result = lax.map(one_group, (features.reshape(GROUPS, FR_GRP, D), line_lengths.reshape(GROUPS, -1), student_logits.reshape(GROUPS, FR_GRP, V)))
    return result.reshape(-1)
```

```python
import functools

import jax
import jax.numpy as jnp
from jax import lax
from jax.experimental import pallas as pl
from jax.experimental.pallas import tpu as pltpu
from jax.sharding import PartitionSpec as P

MESH = pl.DeviceIdType.MESH
EPS = 1e-06
LOW = -1e30

SEND = [[1145178151, 1145210912, -2143288798, 285575176, 268435522], [143163520, 537150477, 134351052, 738197508, 18902028], [-2130697968, 135795072, 109347089, 11534370, 75792688], [839128576, 312475728, 1879049216, -2113915455, -2147347840], [3227712, -2130632192, 20537344, 1078608384, 1784152065]]
DEPTH = [[-1515890086, 169805820, -459392], [-1515890086, 308103670, -870624], [-1515890086, 1374756646, -28384052], [-1515890086, -1336335564, 1342098670], [-1515890086, -1581611588, 1581580262]]
DMAX = 6

TREES = 5
STEPS = 27
UNITS = 132
PAIR0, PAIR1 = 3, 16
BASE_B = TREES * STEPS
LAG = 5
BASE = LAG * DMAX
SLOTS = STEPS + BASE


def block_index(u, pair):
    t, k = u % TREES, u // TREES
    return jnp.where(pair == 1, BASE_B + t * PAIR1 + k, t * STEPS + k)


def kernel(
    root, lens, feats, student, pw, up, dn, cl, ck_in, ng_in, out,
    w, sv, feat, lhs, resid, acc, tmx, tsm, tcr, smx, sse, stat, rcv, ck, ng, role,
    recv, sent, pair_sent, pair_recv, load, par_recv, par_sent, fin_sent, fin_recv,
    st_sent, st_recv,
):
    g, c = lax.axis_index("group"), lax.axis_index("cls")
    x, y, zl = g % 4, (g // 4) % 4, g // 16
    core, zh = c % 2, c // 2
    rel = (x + 4 - root % 4) % 4 + 4 * ((y + 4 - (root // 4) % 4) % 4) + 16 * ((zl + 2 - root // 16) % 2)
    at = lambda zz, yy, xx: zz * 16 + yy * 4 + xx
    near = [
        at(zl, y, (x + 1) % 4), at(zl, y, (x + 3) % 4),
        at(zl, (y + 1) % 4, x), at(zl, (y + 3) % 4, x), at(1 - zl, y, x),
    ]
    peer = lambda j: ((zh + j // 2) % 2) * 2 + (core + j % 2) % 2

    barrier = pltpu.get_barrier_semaphore()
    for d in range(5):
        pl.semaphore_signal(barrier, inc=1, device_id=(near[d], c), device_id_type=MESH)
    for j in range(1, 4):
        pl.semaphore_signal(barrier, inc=1, device_id=(g, peer(j)), device_id_type=MESH)

    def local(src, u):
        t, k = u % TREES, u // TREES
        pltpu.make_async_copy(src, w.at[t * STEPS + k], recv.at[t, k]).start()

    @pl.when(rel == 0)
    def _():
        pltpu.make_async_copy(ck_in, ck, par_recv.at[0]).start()
        pltpu.make_async_copy(ng_in, ng, par_recv.at[1]).start()

        @pl.loop(0, 16)
        def _(u):
            local(pw.at[0, pl.ds((u % 4) * 128, 128), pl.ds(pl.multiple_of((u // 4) * 128, 128), 128)], u)

        @pl.loop(0, 64)
        def _(v):
            r = v % 32
            base = (core * 2 + v // 32) * 512
            across = pl.multiple_of(((r % 16) // 4) * 128, 128)

            @pl.when(r < 16)
            def _():
                local(up.at[0, pl.ds((r % 4) * 128, 128), pl.ds(pl.multiple_of(base + across, 128), 128)], 16 + v)

            @pl.when(r >= 16)
            def _():
                local(dn.at[0, pl.ds(pl.multiple_of(base + (r % 4) * 128, 128), 128), pl.ds(across, 128)], 16 + v)

        @pl.loop(0, 52)
        def _(v):
            local(cl.at[0, pl.ds((v % 4) * 128, 128), pl.ds(pl.multiple_of((v // 4) * 128, 128), 128)], 80 + v)

    load_feat = pltpu.make_async_copy(feats, feat, load.at[0])
    load_stud = pltpu.make_async_copy(student, sv, load.at[1])
    load_feat.start()
    load_stud.start()

    bit = lambda m: lax.shift_right_logical(jnp.int32(m), rel) & 1
    for t in range(TREES):
        role[t] = LAG * (bit(DEPTH[t][0]) + 2 * bit(DEPTH[t][1]) + 4 * bit(DEPTH[t][2]))
        for d in range(5):
            role[8 + t * 5 + d] = bit(SEND[t][d])

    tmx[...] = jnp.full(tmx.shape, LOW, jnp.float32)
    tsm[...] = jnp.zeros(tsm.shape, jnp.float32)
    tcr[...] = jnp.zeros(tcr.shape, jnp.float32)
    pl.semaphore_wait(barrier, 8)

    def forward(s):
        @pl.when(s == role[0])
        def _():
            for i, ref in enumerate((ck, ng)):
                pltpu.make_async_copy(ref, ref, par_recv.at[i]).wait()
                for d in range(5):
                    @pl.when(role[8 + d] == 1)
                    def _():
                        pltpu.make_async_remote_copy(
                            ref, ref, par_sent.at[i, d], par_recv.at[i],
                            device_id=(near[d], c), device_id_type=MESH,
                        ).start()

        @pl.loop(0, TREES)
        def _(t):
            k = s - role[t]
            steps = jnp.where(t < UNITS - TREES * (STEPS - 1), STEPS, STEPS - 1)

            @pl.when((k >= 0) & (k < steps))
            def _():
                block = w.at[t * STEPS + k]
                pltpu.make_async_copy(block, block, recv.at[t, k]).wait()
                for d in range(5):
                    @pl.when(role[8 + t * 5 + d] == 1)
                    def _():
                        pltpu.make_async_remote_copy(
                            block, block, sent.at[t, d], recv.at[t, k],
                            device_id=(near[d], c), device_id_type=MESH,
                        ).start()

                @pl.when((k >= PAIR0) & (k < PAIR1))
                def _():
                    pltpu.make_async_remote_copy(
                        block, w.at[BASE_B + t * PAIR1 + k], pair_sent.at[t], pair_recv.at[t, k],
                        device_id=(g, peer(1)), device_id_type=MESH,
                    ).start()

    def product(l, u, pair):
        columns = []
        for b in range(2):
            rows = [w[block_index(jnp.minimum(u + 4 * b + i, UNITS - 4 + i), pair)] for i in range(4)]
            columns.append(jnp.concatenate(rows, axis=0))
        acc[...] = jnp.dot(
            lhs[l], jnp.concatenate(columns, axis=1), preferred_element_type=jnp.float32
        )

    def student_stats(n):
        @pl.loop(0, 4)
        def _(p):
            v = sv[pl.ds(pl.multiple_of(n * 128 + p * 32, 32), 32), :].astype(jnp.float32)
            parts = [v[:, 128 * i : 128 * (i + 1)] for i in range(13)]
            top = functools.reduce(jnp.maximum, parts)
            here = pl.ds(pl.multiple_of(p * 32, 32), 32)
            smx[here, :] = top
            sse[here, :] = sum(jnp.exp(q - top) for q in parts)

        top = smx[...].T
        peak = jnp.max(top, axis=0, keepdims=True)
        total = jnp.sum(sse[...].T * jnp.exp(top - peak), axis=0, keepdims=True)
        lanes = pl.ds(pl.multiple_of((n % 2) * 128, 128), 128)
        stat[n // 2, 3:4, lanes] = peak
        stat[n // 2, 4:5, lanes] = total

    def convolve():
        rows = lax.broadcasted_iota(jnp.int32, (256, 128), 0)
        keep = rows < lens[0]

        @pl.loop(0, 4)
        def _(q):
            lanes = pl.ds(pl.multiple_of(q * 128, 128), 128)
            v = feat[:, lanes].astype(jnp.float32)
            m = jnp.where(keep, v, 0.0)
            before = jnp.where(rows == 0, 0.0, pltpu.roll(m, 1, 0))
            after = jnp.where(rows == 255, 0.0, pltpu.roll(m, 255, 0))
            k = ck[0, :, lanes].astype(jnp.float32)
            mixed = k[0:1] * before + k[1:2] * m + k[2:3] * after
            lhs[4, :, lanes] = mixed.astype(jnp.bfloat16)
            resid[:, lanes] = v

    def normalize(dest, gain):
        gains = ng[0].astype(jnp.float32)[gain : gain + 1]

        @pl.loop(0, 8)
        def _(p):
            here = pl.ds(pl.multiple_of(p * 32, 32), 32)
            v = resid[here, :]
            scale = lax.rsqrt(jnp.mean(v * v, axis=-1, keepdims=True) + EPS)
            lhs[dest, here, :] = (v * scale * gains).astype(jnp.bfloat16)

    def granule(kind, l, u, pair, half, j):
        product(l, u, pair)
        lanes = pl.ds(pl.multiple_of(half * 256, 256), 256)

        @pl.when(kind == 0)
        def _():
            @pl.loop(0, 4)
            def _(p):
                here = pl.ds(pl.multiple_of(p * 64, 64), 64)
                resid[here, lanes] += acc[here, :]

        @pl.when(kind == 1)
        def _():
            @pl.loop(0, 4)
            def _(p):
                here = pl.ds(pl.multiple_of(p * 64, 64), 64)
                lhs[5, here, lanes] = jax.nn.gelu(acc[here, :]).astype(jnp.bfloat16)

        @pl.when(kind == 2)
        def _():
            first = pl.ds(pl.multiple_of(half * 256, 128), 128)
            second = pl.ds(pl.multiple_of(jnp.minimum(half * 256 + 128, 1536), 128), 128)

            @pl.loop(0, 4)
            def _(p):
                here = pl.ds(pl.multiple_of(p * 64, 64), 64)
                t = acc[here, :].astype(jnp.bfloat16).astype(jnp.float32)
                t0 = t[:, :128]
                t1 = jnp.where(half < 6, t[:, 128:], LOW)
                rows = pl.ds(pl.multiple_of(peer(j) * 256 + p * 64, 64), 64)
                s0 = sv[rows, first].astype(jnp.float32)
                s1 = sv[rows, second].astype(jnp.float32)
                old = tmx[rows, :]
                new = jnp.maximum(old, jnp.maximum(t0, t1))
                fade = jnp.exp(old - new)
                e0, e1 = jnp.exp(t0 - new), jnp.exp(t1 - new)
                tmx[rows, :] = new
                tsm[rows, :] = tsm[rows, :] * fade + (e0 + e1)
                tcr[rows, :] = tcr[rows, :] * fade + (e0 * (t0 - s0) + e1 * (t1 - s1))

    def ready(n):
        n = jnp.where(n >= STEPS - 1, 7, jnp.maximum((TREES * (n + 1) - 80) // 8, 0))
        return n

    def share(i, l, dest, j):
        return pltpu.make_async_remote_copy(
            lhs.at[l], lhs.at[dest], fin_sent.at[i], fin_recv.at[i],
            device_id=(g, peer(j)), device_id_type=MESH,
        )

    @pl.loop(0, SLOTS)
    def _(s):
        forward(s)
        n = s - BASE

        @pl.when(s == 0)
        def _():
            load_feat.wait()
            load_stud.wait()

        @pl.when((s >= 1) & (s < 9))
        def _():
            student_stats(s - 1)

        @pl.when((n > PAIR0) & (n <= PAIR1))
        def _():
            @pl.loop(0, TREES)
            def _(t):
                block = w.at[BASE_B + t * PAIR1 + n - 1]
                pltpu.make_async_copy(block, block, pair_recv.at[t, n - 1]).wait()

        @pl.when(n == 0)
        def _():
            convolve()

        chunk = jnp.where(n == 10, 0, jnp.where(n == 12, 1, jnp.where(n == 16, 2, 3)))
        chunks = (n == 10) | (n == 12) | (n == 16) | (n == 17)
        count = jnp.where(n == 4, 2, jnp.where(chunks, 4, 0))

        def due(i, _):
            first = n == 4
            kind = jnp.where(first | (i >= 2), 0, 1)
            l = jnp.where(first | (i < 2), 4, 5)
            u = jnp.where(first, 8 * i, 16 + 32 * (chunk // 2) + 8 * i)
            pair = jnp.where(first, 0, chunk % 2)
            return kind, l, u, pair, i % 2, 0

        starts = (18, 20, 23, 25)
        los, his = [], []
        for j in range(4):
            los.append(jnp.where(n - 1 >= starts[j], ready(n - 1), 0))
            his.append(jnp.where(n >= starts[j], ready(n), 0))

        @pl.when(n == 20)
        def _():
            share(0, 1, 1, 1).wait_recv()

        @pl.when(n == 23)
        def _():
            share(1, 2, 2, 2).wait_recv()
            share(2, 2, 3, 1).start()

        @pl.when(n == 25)
        def _():
            share(2, 3, 3, 1).wait_recv()

        sizes = [his[j] - los[j] for j in range(4)]
        ends = [sizes[0], sizes[0] + sizes[1], sizes[0] + sizes[1] + sizes[2]]
        total = ends[2] + sizes[3]

        def step(i, _):
            q = i - count
            j = jnp.where(q < ends[0], 0, jnp.where(q < ends[1], 1, jnp.where(q < ends[2], 2, 3)))
            start = jnp.where(
                q < ends[0], los[0],
                jnp.where(q < ends[1], los[1] - ends[0], jnp.where(q < ends[2], los[2] - ends[1], los[3] - ends[2])),
            )
            slab = q + start
            cls = i >= count
            kind, l, u, pair, half, _z = due(i, 0)
            granule(
                jnp.where(cls, 2, kind), jnp.where(cls, j, l), jnp.where(cls, 80 + 8 * slab, u),
                jnp.where(cls, 0, pair), jnp.where(cls, slab, half), j,
            )
            return 0

        lax.fori_loop(0, count + total, step, 0)

        @pl.when(n == 4)
        def _():
            normalize(4, 0)

        @pl.when(n == 17)
        def _():
            normalize(0, 1)
            share(0, 0, 1, 1).start()
            share(1, 0, 2, 2).start()

    def tell(j):
        return pltpu.make_async_remote_copy(
            stat.at[peer(j)], rcv.at[j], st_sent.at[j], st_recv.at[j],
            device_id=(g, peer(j)), device_id_type=MESH,
        )

    @pl.loop(0, 8)
    def _(i):
        j, h = 3 - i // 2, i % 2
        rows = pl.ds(pl.multiple_of(peer(j) * 256 + h * 128, 128), 128)
        top = tmx[rows, :].T
        peak = jnp.max(top, axis=0, keepdims=True)
        fade = jnp.exp(top - peak)
        lanes = pl.ds(pl.multiple_of(h * 128, 128), 128)
        b = peer(j)
        stat[b, 0:1, lanes] = peak
        stat[b, 1:2, lanes] = jnp.sum(tsm[rows, :].T * fade, axis=0, keepdims=True)
        stat[b, 2:3, lanes] = jnp.sum(tcr[rows, :].T * fade, axis=0, keepdims=True)

        @pl.when((h == 1) & (j > 0))
        def _():
            tell(j).start()

    for i, (l, dest, j) in enumerate(((0, 1, 1), (0, 2, 2), (2, 3, 1))):
        share(i, l, dest, j).wait_send()

    @pl.loop(0, TREES)
    def _(t):
        for d in range(5):
            for steps in (STEPS, STEPS - 1):
                whole = t < UNITS - TREES * (STEPS - 1)
                @pl.when((role[8 + t * 5 + d] == 1) & (whole if steps == STEPS else jnp.logical_not(whole)))
                def _():
                    part = w.at[pl.ds(t * STEPS, steps)]
                    pltpu.make_async_copy(part, part, sent.at[t, d]).wait()
        part = w.at[pl.ds(BASE_B + t * PAIR1 + PAIR0, PAIR1 - PAIR0)]
        pltpu.make_async_copy(part, part, pair_sent.at[t]).wait()

    for i, ref in enumerate((ck, ng)):
        for d in range(5):
            @pl.when(role[8 + d] == 1)
            def _():
                pltpu.make_async_copy(ref, ref, par_sent.at[i, d]).wait()

    for j in range(1, 4):
        tell(j).wait()
    rcv[0] = stat[c]
    got = [rcv[j] for j in range(4)]
    tm = functools.reduce(jnp.maximum, [r[0:1] for r in got])
    sm = functools.reduce(jnp.maximum, [r[3:4] for r in got])
    tw = [jnp.exp(r[0:1] - tm) for r in got]
    ts = sum(r[1:2] * f for r, f in zip(got, tw))
    tc = sum(r[2:3] * f for r, f in zip(got, tw))
    ss = sum(r[4:5] * jnp.exp(r[3:4] - sm) for r in got)
    value = tc / ts - (tm + jnp.log(ts)) + (sm + jnp.log(ss))
    lane = lax.broadcasted_iota(jnp.int32, (1, 256), 1)
    out[...] = jnp.where(lane < lens[0], value, 0.0)


def call(root, *operands):
    hbm = pl.BlockSpec(memory_space=pl.ANY)
    f32, bf16 = jnp.float32, jnp.bfloat16
    dma = pltpu.SemaphoreType.DMA
    return pl.pallas_call(
        functools.partial(kernel, root),
        out_shape=jax.ShapeDtypeStruct((1, 256), f32),
        in_specs=[pl.BlockSpec(memory_space=pltpu.SMEM)] + [hbm] * 8,
        out_specs=pl.BlockSpec(memory_space=pltpu.VMEM),
        scratch_shapes=[
            pltpu.VMEM((BASE_B + TREES * PAIR1, 128, 128), bf16),
            pltpu.VMEM((1024, 1664), bf16),
            pltpu.VMEM((256, 512), bf16),
            pltpu.VMEM((6, 256, 512), bf16),
            pltpu.VMEM((256, 512), f32),
            pltpu.VMEM((256, 256), f32),
            pltpu.VMEM((1024, 128), f32),
            pltpu.VMEM((1024, 128), f32),
            pltpu.VMEM((1024, 128), f32),
            pltpu.VMEM((128, 128), f32),
            pltpu.VMEM((128, 128), f32),
            pltpu.VMEM((4, 8, 256), f32),
            pltpu.VMEM((4, 8, 256), f32),
            pltpu.VMEM((1, 3, 512), bf16),
            pltpu.VMEM((1, 2, 512), bf16),
            pltpu.SMEM((40,), jnp.int32),
            dma((TREES, STEPS)),
            dma((TREES, 5)),
            dma((TREES,)),
            dma((TREES, PAIR1)),
            dma((2,)),
            dma((2,)),
            dma((2, 5)),
            dma((3,)),
            dma((3,)),
            dma((4,)),
            dma((4,)),
        ],
        compiler_params=pltpu.CompilerParams(collective_id=root, has_side_effects=True),
        name=f"teach{root}",
    )(*operands)


def body(features, student, lengths, source, pw, up, dn, cl, ck, ng):
    branches = [functools.partial(call, root) for root in range(pw_groups)]
    result = lax.switch(source[0], branches, lengths, features, student, pw, up, dn, cl, ck, ng)
    return result.reshape(256)


pw_groups = 32


def solution(mesh):
    return jax.shard_map(
        body,
        mesh=mesh,
        in_specs=(
            P(("group", "cls"), None),
            P("group", "cls"),
            P(("group", "cls")),
            P(),
            P("group", None, None),
            P("group", None, None),
            P("group", None, None),
            P("group", None, "cls"),
            P("group", None, None),
            P("group", None, None),
        ),
        out_specs=P(("group", "cls")),
        check_vma=False,
    )
```

```python
import functools

import jax
import jax.numpy as jnp
from jax import lax
from jax.experimental import pallas as pl
from jax.experimental.pallas import tpu as pltpu
from jax.sharding import PartitionSpec as P

MESH = pl.DeviceIdType.MESH
EPS = 1e-06
LOW = -1e30

SEND = [[1145178151, 1145210912, -2143288798, 285575176, 268435522], [143163520, 537150477, 134351052, 738197508, 18902028], [-2130697968, 135795072, 109347089, 11534370, 75792688], [839128576, 312475728, 1879049216, -2113915455, -2147347840], [3227712, -2130632192, 20537344, 1078608384, 1784152065]]
DEPTH = [[-1515890086, 169805820, -459392], [-1515890086, 308103670, -870624], [-1515890086, 1374756646, -28384052], [-1515890086, -1336335564, 1342098670], [-1515890086, -1581611588, 1581580262]]
DMAX = 6

TREES = 5
STEPS = 14
UNITS = 66
PAIR0, PAIR1 = 1, 8
BASE_B = TREES * STEPS
LAG = 3
BASE = LAG * DMAX
SLOTS = STEPS + BASE
STUDENT = 2


def block_index(u, pair):
    t, k = u % TREES, u // TREES
    return jnp.where(pair == 1, BASE_B + t * PAIR1 + k, t * STEPS + k)


def kernel(*refs):
    dma = pltpu.SemaphoreType.DMA
    pl.run_scoped(
        functools.partial(scoped, *refs),
        dma((TREES, STEPS)), dma((TREES, 5)), dma((TREES,)), dma((TREES, PAIR1)), dma((2,)), dma((2,)),
        dma((2, 5)), dma((3,)), dma((3,)), dma((4,)), dma((4,)),
    )


def scoped(
    root, lens, feats, student, pw, up, dn, cl, ck_in, ng_in, out,
    w, sv, feat, lhs, resid, acc, tops, sums, tcr, stat, rcv, ck, ng, role,
    recv, sent, pair_sent, pair_recv, load, par_recv, par_sent, fin_sent, fin_recv,
    st_sent, st_recv,
):
    g, c = lax.axis_index("group"), lax.axis_index("cls")
    x, y, zl = g % 4, (g // 4) % 4, g // 16
    core, zh = c % 2, c // 2
    rel = (x + 4 - root % 4) % 4 + 4 * ((y + 4 - (root // 4) % 4) % 4) + 16 * ((zl + 2 - root // 16) % 2)
    at = lambda zz, yy, xx: zz * 16 + yy * 4 + xx
    near = [
        at(zl, y, (x + 1) % 4), at(zl, y, (x + 3) % 4),
        at(zl, (y + 1) % 4, x), at(zl, (y + 3) % 4, x), at(1 - zl, y, x),
    ]
    peer = lambda j: ((zh + j // 2) % 2) * 2 + (core + j % 2) % 2

    barrier = pltpu.get_barrier_semaphore()
    for d in range(5):
        pl.semaphore_signal(barrier, inc=1, device_id=(near[d], c), device_id_type=MESH)
    for j in range(1, 4):
        pl.semaphore_signal(barrier, inc=1, device_id=(g, peer(j)), device_id_type=MESH)

    def local(src, u):
        t, k = u % TREES, u // TREES
        pltpu.make_async_copy(src, w.at[t * STEPS + k], recv.at[t, k]).start()

    @pl.when(rel == 0)
    def _():
        pltpu.make_async_copy(ck_in, ck, par_recv.at[0]).start()
        pltpu.make_async_copy(ng_in, ng, par_recv.at[1]).start()

        @pl.loop(0, 8)
        def _(u):
            local(pw.at[0, pl.ds((u % 2) * 256, 256), pl.ds(pl.multiple_of((u // 2) * 128, 128), 128)], u)

        @pl.loop(0, 32)
        def _(v):
            r = v % 16
            base = (core * 2 + v // 16) * 512
            across = pl.multiple_of(((r % 8) // 2) * 128, 128)

            @pl.when(r < 8)
            def _():
                local(up.at[0, pl.ds((r % 2) * 256, 256), pl.ds(pl.multiple_of(base + across, 128), 128)], 8 + v)

            @pl.when(r >= 8)
            def _():
                local(dn.at[0, pl.ds(pl.multiple_of(base + (r % 2) * 256, 128), 256), pl.ds(across, 128)], 8 + v)

        @pl.loop(0, 30)
        def _(i):
            v = jnp.where(i < 26, i, i - 4)
            local(cl.at[0, pl.ds((v % 2) * 256, 256), pl.ds(pl.multiple_of((v // 2) * 128, 128), 128)], 40 + i)

    load_feat = pltpu.make_async_copy(feats, feat, load.at[0])
    load_stud = pltpu.make_async_copy(student, sv, load.at[1])
    load_feat.start()
    load_stud.start()

    bit = lambda m: lax.shift_right_logical(jnp.int32(m), rel) & 1
    for t in range(TREES):
        role[t] = LAG * (bit(DEPTH[t][0]) + 2 * bit(DEPTH[t][1]) + 4 * bit(DEPTH[t][2]))
        count = jnp.int32(0)
        for d in range(5):
            role[16 + t * 5 + count] = near[d]
            count += bit(SEND[t][d])
        role[8 + t] = count

    @pl.loop(0, 16)
    def _(p):
        here = pl.ds(pl.multiple_of(p * 64, 64), 64)
        tops[0, here, :] = jnp.full((64, 128), LOW, jnp.float32)
        sums[0, here, :] = jnp.zeros((64, 128), jnp.float32)
        tcr[here, :] = jnp.zeros((64, 128), jnp.float32)

    pl.semaphore_wait(barrier, 8)

    def forward(s):
        @pl.when(s == role[0])
        def _():
            for i, ref in enumerate((ck, ng)):
                pltpu.make_async_copy(ref, ref, par_recv.at[i]).wait()

            @pl.loop(0, role[8])
            def _(d):
                for i, ref in enumerate((ck, ng)):
                    pltpu.make_async_remote_copy(
                        ref, ref, par_sent.at[i, d], par_recv.at[i],
                        device_id=(role[16 + d], c), device_id_type=MESH,
                    ).start()

        @pl.loop(0, TREES)
        def _(t):
            k = s - role[t]

            @pl.when((k >= 0) & (k < STEPS))
            def _():
                block = w.at[t * STEPS + k]
                pltpu.make_async_copy(block, block, recv.at[t, k]).wait()

                @pl.loop(0, role[8 + t])
                def _(d):
                    pltpu.make_async_remote_copy(
                        block, block, sent.at[t, d], recv.at[t, k],
                        device_id=(role[16 + t * 5 + d], c), device_id_type=MESH,
                    ).start()

                @pl.when((k >= PAIR0) & (k < PAIR1))
                def _():
                    pltpu.make_async_remote_copy(
                        block, w.at[BASE_B + t * PAIR1 + k], pair_sent.at[t], pair_recv.at[t, k],
                        device_id=(g, peer(1)), device_id_type=MESH,
                    ).start()

    def product(l, u, pair):
        columns = []
        for b in range(2):
            rows = [w[block_index(jnp.minimum(u + 2 * b + i, UNITS - 2 + i), pair)] for i in range(2)]
            columns.append(jnp.concatenate(rows, axis=0))
        acc[...] = jnp.dot(
            lhs[l], jnp.concatenate(columns, axis=1), preferred_element_type=jnp.float32
        )

    def student_stats(n):
        @pl.loop(0, 4)
        def _(p):
            here = pl.ds(pl.multiple_of(n * 64 + p * 16, 16), 16)
            v = sv[here, :].astype(jnp.float32)
            parts = [v[:, 128 * i : 128 * (i + 1)] for i in range(13)]
            top = functools.reduce(jnp.maximum, parts)
            tops[1, here, :] = top
            sums[1, here, :] = sum(jnp.exp(q - top) for q in parts)

    def tell(j):
        return pltpu.make_async_remote_copy(
            stat.at[peer(j)], rcv.at[j], st_sent.at[j], st_recv.at[j],
            device_id=(g, peer(j)), device_id_type=MESH,
        )

    def gather_stats(kind, i):
        j, h = 3 - i // 2, i % 2
        b = peer(j)
        rows = pl.ds(pl.multiple_of(b * 256 + h * 128, 128), 128)
        top = tops[kind, rows, :].T
        peak = jnp.max(top, axis=0, keepdims=True)
        fade = jnp.exp(top - peak)
        lanes = pl.ds(pl.multiple_of(h * 128, 128), 128)
        stat[b, kind, 0:1, lanes] = peak
        stat[b, kind, 1:2, lanes] = jnp.sum(sums[kind, rows, :].T * fade, axis=0, keepdims=True)
        stat[b, kind, 2:3, lanes] = jnp.sum(tcr[rows, :].T * fade, axis=0, keepdims=True)

        @pl.when((kind == 0) & (h == 1) & (j > 0))
        def _():
            tell(j).start()

    def convolve():
        rows = lax.broadcasted_iota(jnp.int32, (256, 128), 0)
        keep = rows < lens[0]

        @pl.loop(0, 4)
        def _(q):
            lanes = pl.ds(pl.multiple_of(q * 128, 128), 128)
            v = feat[:, lanes].astype(jnp.float32)
            m = jnp.where(keep, v, 0.0)
            before = jnp.where(rows == 0, 0.0, pltpu.roll(m, 1, 0))
            after = jnp.where(rows == 255, 0.0, pltpu.roll(m, 255, 0))
            k = ck[0, :, lanes].astype(jnp.float32)
            mixed = k[0:1] * before + k[1:2] * m + k[2:3] * after
            lhs[4, :, lanes] = mixed.astype(jnp.bfloat16)
            resid[:, lanes] = v

    def normalize(dest, gain):
        gains = ng[0].astype(jnp.float32)[gain : gain + 1]

        @pl.loop(0, 8)
        def _(p):
            here = pl.ds(pl.multiple_of(p * 32, 32), 32)
            v = resid[here, :]
            scale = lax.rsqrt(jnp.mean(v * v, axis=-1, keepdims=True) + EPS)
            lhs[dest, here, :] = (v * scale * gains).astype(jnp.bfloat16)

    def granule(kind, l, u, pair, half, j):
        product(l, u, pair)
        lanes = pl.ds(pl.multiple_of(half * 256, 256), 256)

        @pl.when(kind == 0)
        def _():
            @pl.loop(0, 4)
            def _(p):
                here = pl.ds(pl.multiple_of(p * 64, 64), 64)
                resid[here, lanes] += acc[here, :]

        @pl.when(kind == 1)
        def _():
            @pl.loop(0, 4)
            def _(p):
                here = pl.ds(pl.multiple_of(p * 64, 64), 64)
                lhs[5, here, lanes] = jax.nn.gelu(acc[here, :]).astype(jnp.bfloat16)

        @pl.when(kind == 2)
        def _():
            first = pl.ds(pl.multiple_of(half * 256, 128), 128)
            second = pl.ds(pl.multiple_of(jnp.minimum(half * 256 + 128, 1536), 128), 128)

            @pl.loop(0, 4)
            def _(p):
                here = pl.ds(pl.multiple_of(p * 64, 64), 64)
                t = acc[here, :].astype(jnp.bfloat16).astype(jnp.float32)
                t0 = t[:, :128]
                t1 = jnp.where(half < 6, t[:, 128:], LOW)
                rows = pl.ds(pl.multiple_of(peer(j) * 256 + p * 64, 64), 64)
                s0 = sv[rows, first].astype(jnp.float32)
                s1 = sv[rows, second].astype(jnp.float32)
                old = tops[0, rows, :]
                new = jnp.maximum(old, jnp.maximum(t0, t1))
                fade = jnp.exp(old - new)
                e0, e1 = jnp.exp(t0 - new), jnp.exp(t1 - new)
                tops[0, rows, :] = new
                sums[0, rows, :] = sums[0, rows, :] * fade + (e0 + e1)
                tcr[rows, :] = tcr[rows, :] * fade + (e0 * (t0 - s0) + e1 * (t1 - s1))

    def ready(n):
        n = jnp.clip((TREES * (n + 1) - 40) // 4, 0, 7)
        return n

    def share(i, l, dest, j):
        return pltpu.make_async_remote_copy(
            lhs.at[l], lhs.at[dest], fin_sent.at[i], fin_recv.at[i],
            device_id=(g, peer(j)), device_id_type=MESH,
        )

    @pl.loop(0, SLOTS + 8)
    def _(s):
        forward(s)
        n = s - BASE

        @pl.when(s == STUDENT)
        def _():
            load_feat.wait()
            load_stud.wait()

        @pl.when((s >= STUDENT) & (s < STUDENT + 16))
        def _():
            student_stats(s - STUDENT)

        student = (s >= STUDENT + 16) & (s < STUDENT + 24)
        late = s >= SLOTS
        @pl.when(student | late)
        def _():
            gather_stats(jnp.where(late, 0, 1), jnp.where(late, s - SLOTS, s - STUDENT - 16))

        @pl.when((n > PAIR0) & (n <= PAIR1))
        def _():
            @pl.loop(0, TREES)
            def _(t):
                block = w.at[BASE_B + t * PAIR1 + n - 1]
                pltpu.make_async_copy(block, block, pair_recv.at[t, n - 1]).wait()

        @pl.when(n == 0)
        def _():
            convolve()

        chunk = jnp.where(n == 4, 0, jnp.where(n == 5, 1, jnp.where(n == 7, 2, 3)))
        chunks = (n == 4) | (n == 5) | (n == 7) | (n == 8)
        count = jnp.where(n == 1, 2, jnp.where(chunks, 4, 0))

        def due(i, _):
            first = n == 1
            kind = jnp.where(first | (i >= 2), 0, 1)
            l = jnp.where(first | (i < 2), 4, 5)
            u = jnp.where(first, 4 * i, 8 + 16 * (chunk // 2) + 4 * i)
            pair = jnp.where(first, 0, chunk % 2)
            return kind, l, u, pair, i % 2, 0

        starts = (9, 10, 12, 13)
        los, his = [], []
        for j in range(4):
            los.append(jnp.where(n - 1 >= starts[j], ready(n - 1), 0))
            his.append(jnp.where(n >= starts[j], ready(n), 0))

        @pl.when(n == 10)
        def _():
            share(0, 1, 1, 1).wait_recv()

        @pl.when(n == 12)
        def _():
            share(1, 2, 2, 2).wait_recv()
            share(2, 2, 3, 1).start()

        @pl.when(n == 13)
        def _():
            share(2, 3, 3, 1).wait_recv()

        sizes = [his[j] - los[j] for j in range(4)]
        ends = [sizes[0], sizes[0] + sizes[1], sizes[0] + sizes[1] + sizes[2]]
        total = ends[2] + sizes[3]

        def step(i, _):
            q = i - count
            j = jnp.where(q < ends[0], 0, jnp.where(q < ends[1], 1, jnp.where(q < ends[2], 2, 3)))
            start = jnp.where(
                q < ends[0], los[0],
                jnp.where(q < ends[1], los[1] - ends[0], jnp.where(q < ends[2], los[2] - ends[1], los[3] - ends[2])),
            )
            slab = q + start
            cls = i >= count
            kind, l, u, pair, half, _z = due(i, 0)
            granule(
                jnp.where(cls, 2, kind), jnp.where(cls, j, l), jnp.where(cls, 40 + 4 * slab, u),
                jnp.where(cls, 0, pair), jnp.where(cls, slab, half), j,
            )
            return 0

        lax.fori_loop(0, count + total, step, 0)

        @pl.when(n == 1)
        def _():
            normalize(4, 0)

        @pl.when(n == 8)
        def _():
            normalize(0, 1)
            share(0, 0, 1, 1).start()
            share(1, 0, 2, 2).start()

    for i, (l, dest, j) in enumerate(((0, 1, 1), (0, 2, 2), (2, 3, 1))):
        share(i, l, dest, j).wait_send()

    @pl.loop(0, TREES)
    def _(t):
        @pl.loop(0, role[8 + t])
        def _(d):
            part = w.at[pl.ds(t * STEPS, STEPS)]
            pltpu.make_async_copy(part, part, sent.at[t, d]).wait()

        part = w.at[pl.ds(BASE_B + t * PAIR1 + PAIR0, PAIR1 - PAIR0)]
        pltpu.make_async_copy(part, part, pair_sent.at[t]).wait()

    @pl.loop(0, role[8])
    def _(d):
        for i, ref in enumerate((ck, ng)):
            pltpu.make_async_copy(ref, ref, par_sent.at[i, d]).wait()

    for j in range(1, 4):
        tell(j).wait()
    rcv[0] = stat[c]
    got = [jnp.concatenate([rcv[j, 0, 0:3], rcv[j, 1, 0:2]], axis=0) for j in range(4)]
    tm = functools.reduce(jnp.maximum, [r[0:1] for r in got])
    sm = functools.reduce(jnp.maximum, [r[3:4] for r in got])
    tw = [jnp.exp(r[0:1] - tm) for r in got]
    ts = sum(r[1:2] * f for r, f in zip(got, tw))
    tc = sum(r[2:3] * f for r, f in zip(got, tw))
    ss = sum(r[4:5] * jnp.exp(r[3:4] - sm) for r in got)
    value = tc / ts - (tm + jnp.log(ts)) + (sm + jnp.log(ss))
    lane = lax.broadcasted_iota(jnp.int32, (1, 256), 1)
    out[...] = jnp.where(lane < lens[0], value, 0.0)


def call(root, *operands):
    hbm = pl.BlockSpec(memory_space=pl.ANY)
    f32, bf16 = jnp.float32, jnp.bfloat16
    return pl.pallas_call(
        functools.partial(kernel, root),
        out_shape=jax.ShapeDtypeStruct((1, 256), f32),
        in_specs=[pl.BlockSpec(memory_space=pltpu.SMEM)] + [hbm] * 8,
        out_specs=pl.BlockSpec(memory_space=pltpu.VMEM),
        scratch_shapes=[
            pltpu.VMEM((BASE_B + TREES * PAIR1, 256, 128), bf16),
            pltpu.VMEM((1024, 1664), bf16),
            pltpu.VMEM((256, 512), bf16),
            pltpu.VMEM((6, 256, 512), bf16),
            pltpu.VMEM((256, 512), f32),
            pltpu.VMEM((256, 256), f32),
            pltpu.VMEM((2, 1024, 128), f32),
            pltpu.VMEM((2, 1024, 128), f32),
            pltpu.VMEM((1024, 128), f32),
            pltpu.VMEM((4, 2, 8, 256), f32),
            pltpu.VMEM((4, 2, 8, 256), f32),
            pltpu.VMEM((1, 3, 512), bf16),
            pltpu.VMEM((1, 2, 512), bf16),
            pltpu.SMEM((48,), jnp.int32),
        ],
        compiler_params=pltpu.CompilerParams(collective_id=root, has_side_effects=True),
        name=f"teach{root}",
    )(*operands)


def body(features, student, lengths, source, pw, up, dn, cl, ck, ng):
    branches = [functools.partial(call, root) for root in range(pw_groups)]
    result = lax.switch(source[0], branches, lengths, features, student, pw, up, dn, cl, ck, ng)
    return result.reshape(256)


pw_groups = 32


def solution(mesh):
    return jax.shard_map(
        body,
        mesh=mesh,
        in_specs=(
            P(("group", "cls"), None),
            P("group", "cls"),
            P(("group", "cls")),
            P(),
            P("group", None, None),
            P("group", None, None),
            P("group", None, None),
            P("group", None, "cls"),
            P("group", None, None),
            P("group", None, None),
        ),
        out_specs=P(("group", "cls")),
        check_vma=False,
    )
```

```python
import functools

import jax
import jax.numpy as jnp
from jax import lax
from jax.experimental import pallas as pl
from jax.experimental.pallas import tpu as pltpu
from jax.sharding import PartitionSpec as P

MESH = pl.DeviceIdType.MESH
EPS = 1e-06
LOW = -1e30

SEND = [[1145456199, 572662304, 393254, 6, 26114], [-2004318080, 1153748173, 12582920, 294920, 32908], [304, 135266320, 253759441, 15728864, 2416], [268447744, -1879043840, -268378112, -16744703, 4096], [590413824, 17367040, 1638400, 720896, -131071]]
DEPTH = [[-1515890086, 673673852, -539456128], [-1515890086, -2104633130, 2138187552], [-1515890086, 1102126058, -28384252], [-1515890086, -1321080038, 1325270244], [-1515890086, -1312943078, 1312878564]]
DMAX = 6

TREES = 5
STEPS = 14
UNITS = 66
PAIR0, PAIR1 = 1, 8
BASE_B = TREES * STEPS
LAG = 3
BASE = LAG * DMAX
SLOTS = STEPS + BASE
STUDENT = 2


def block_index(u, pair):
    t, k = u % TREES, u // TREES
    return jnp.where(pair == 1, BASE_B + t * PAIR1 + k, t * STEPS + k)


def kernel(*refs):
    dma = pltpu.SemaphoreType.DMA
    pl.run_scoped(
        functools.partial(scoped, *refs),
        dma((TREES, STEPS)), dma((TREES, 5)), dma((TREES,)), dma((TREES, PAIR1)), dma((2,)), dma((2,)),
        dma((2, 5)), dma((3,)), dma((3,)), dma((4,)), dma((4,)),
    )


def scoped(
    root, lens, feats, student, pw, up, dn, cl, ck_in, ng_in, out,
    w, sv, feat, lhs, resid, acc, tops, sums, tcr, stat, rcv, ck, ng, role,
    recv, sent, pair_sent, pair_recv, load, par_recv, par_sent, fin_sent, fin_recv,
    st_sent, st_recv,
):
    g, c = lax.axis_index("group"), lax.axis_index("cls")
    x, y, zl = g % 4, (g // 4) % 4, g // 16
    core, zh = c % 2, c // 2
    rel = (x + 4 - root % 4) % 4 + 4 * ((y + 4 - (root // 4) % 4) % 4) + 16 * ((zl + 2 - root // 16) % 2)
    at = lambda zz, yy, xx: zz * 16 + yy * 4 + xx
    near = [
        at(zl, y, (x + 1) % 4), at(zl, y, (x + 3) % 4),
        at(zl, (y + 1) % 4, x), at(zl, (y + 3) % 4, x), at(1 - zl, y, x),
    ]
    peer = lambda j: ((zh + j // 2) % 2) * 2 + (core + j % 2) % 2

    barrier = pltpu.get_barrier_semaphore()
    for d in range(5):
        pl.semaphore_signal(barrier, inc=1, device_id=(near[d], c), device_id_type=MESH)
    for j in range(1, 4):
        pl.semaphore_signal(barrier, inc=1, device_id=(g, peer(j)), device_id_type=MESH)

    def local(src, u):
        t, k = u % TREES, u // TREES
        pltpu.make_async_copy(src, w.at[t * STEPS + k], recv.at[t, k]).start()

    @pl.when(rel == 0)
    def _():
        pltpu.make_async_copy(ck_in, ck, par_recv.at[0]).start()
        pltpu.make_async_copy(ng_in, ng, par_recv.at[1]).start()

        @pl.loop(0, 8)
        def _(u):
            local(pw.at[0, pl.ds((u % 2) * 256, 256), pl.ds(pl.multiple_of((u // 2) * 128, 128), 128)], u)

        @pl.loop(0, 32)
        def _(v):
            r = v % 16
            base = (core * 2 + v // 16) * 512
            across = pl.multiple_of(((r % 8) // 2) * 128, 128)

            @pl.when(r < 8)
            def _():
                local(up.at[0, pl.ds((r % 2) * 256, 256), pl.ds(pl.multiple_of(base + across, 128), 128)], 8 + v)

            @pl.when(r >= 8)
            def _():
                local(dn.at[0, pl.ds(pl.multiple_of(base + (r % 2) * 256, 128), 256), pl.ds(across, 128)], 8 + v)

        @pl.loop(0, 30)
        def _(i):
            v = jnp.where(i < 26, i, i - 4)
            local(cl.at[0, pl.ds((v % 2) * 256, 256), pl.ds(pl.multiple_of((v // 2) * 128, 128), 128)], 40 + i)

    load_feat = pltpu.make_async_copy(feats, feat, load.at[0])
    load_stud = pltpu.make_async_copy(student, sv, load.at[1])
    load_feat.start()
    load_stud.start()

    bit = lambda m: lax.shift_right_logical(jnp.int32(m), rel) & 1
    for t in range(TREES):
        role[t] = LAG * (bit(DEPTH[t][0]) + 2 * bit(DEPTH[t][1]) + 4 * bit(DEPTH[t][2]))
        count = jnp.int32(0)
        for d in range(5):
            role[16 + t * 5 + count] = near[d]
            count += bit(SEND[t][d])
        role[8 + t] = count

    @pl.loop(0, 16)
    def _(p):
        here = pl.ds(pl.multiple_of(p * 64, 64), 64)
        tops[0, here, :] = jnp.full((64, 128), LOW, jnp.float32)
        sums[0, here, :] = jnp.zeros((64, 128), jnp.float32)
        tcr[here, :] = jnp.zeros((64, 128), jnp.float32)

    pl.semaphore_wait(barrier, 8)

    def forward(s):
        @pl.when(s == role[0])
        def _():
            for i, ref in enumerate((ck, ng)):
                pltpu.make_async_copy(ref, ref, par_recv.at[i]).wait()

            @pl.loop(0, role[8])
            def _(d):
                for i, ref in enumerate((ck, ng)):
                    pltpu.make_async_remote_copy(
                        ref, ref, par_sent.at[i, d], par_recv.at[i],
                        device_id=(role[16 + d], c), device_id_type=MESH,
                    ).start()

        @pl.loop(0, TREES)
        def _(t):
            k = s - role[t]

            @pl.when((k >= 0) & (k < STEPS))
            def _():
                block = w.at[t * STEPS + k]
                pltpu.make_async_copy(block, block, recv.at[t, k]).wait()

                @pl.loop(0, role[8 + t])
                def _(d):
                    pltpu.make_async_remote_copy(
                        block, block, sent.at[t, d], recv.at[t, k],
                        device_id=(role[16 + t * 5 + d], c), device_id_type=MESH,
                    ).start()

                @pl.when((k >= PAIR0) & (k < PAIR1))
                def _():
                    pltpu.make_async_remote_copy(
                        block, w.at[BASE_B + t * PAIR1 + k], pair_sent.at[t], pair_recv.at[t, k],
                        device_id=(g, peer(1)), device_id_type=MESH,
                    ).start()

    def product(l, u, pair):
        columns = []
        for b in range(2):
            rows = [w[block_index(jnp.minimum(u + 2 * b + i, UNITS - 2 + i), pair)] for i in range(2)]
            columns.append(jnp.concatenate(rows, axis=0))
        acc[...] = jnp.dot(
            lhs[l], jnp.concatenate(columns, axis=1), preferred_element_type=jnp.float32
        )

    def student_stats(n):
        @pl.loop(0, 4)
        def _(p):
            here = pl.ds(pl.multiple_of(n * 64 + p * 16, 16), 16)
            v = sv[here, :].astype(jnp.float32)
            parts = [v[:, 128 * i : 128 * (i + 1)] for i in range(13)]
            top = functools.reduce(jnp.maximum, parts)
            tops[1, here, :] = top
            sums[1, here, :] = sum(jnp.exp(q - top) for q in parts)

    def tell(j):
        return pltpu.make_async_remote_copy(
            stat.at[peer(j)], rcv.at[j], st_sent.at[j], st_recv.at[j],
            device_id=(g, peer(j)), device_id_type=MESH,
        )

    def gather_stats(kind, i):
        j, h = 3 - i // 2, i % 2
        b = peer(j)
        rows = pl.ds(pl.multiple_of(b * 256 + h * 128, 128), 128)
        top = tops[kind, rows, :].T
        peak = jnp.max(top, axis=0, keepdims=True)
        fade = jnp.exp(top - peak)
        lanes = pl.ds(pl.multiple_of(h * 128, 128), 128)
        stat[b, kind, 0:1, lanes] = peak
        stat[b, kind, 1:2, lanes] = jnp.sum(sums[kind, rows, :].T * fade, axis=0, keepdims=True)
        stat[b, kind, 2:3, lanes] = jnp.sum(tcr[rows, :].T * fade, axis=0, keepdims=True)

        @pl.when((kind == 0) & (h == 1) & (j > 0))
        def _():
            tell(j).start()

    def convolve():
        rows = lax.broadcasted_iota(jnp.int32, (256, 128), 0)
        keep = rows < lens[0]

        @pl.loop(0, 4)
        def _(q):
            lanes = pl.ds(pl.multiple_of(q * 128, 128), 128)
            v = feat[:, lanes].astype(jnp.float32)
            m = jnp.where(keep, v, 0.0)
            before = jnp.where(rows == 0, 0.0, pltpu.roll(m, 1, 0))
            after = jnp.where(rows == 255, 0.0, pltpu.roll(m, 255, 0))
            k = ck[0, :, lanes].astype(jnp.float32)
            mixed = k[0:1] * before + k[1:2] * m + k[2:3] * after
            lhs[4, :, lanes] = mixed.astype(jnp.bfloat16)
            resid[:, lanes] = v

    def normalize(dest, gain):
        gains = ng[0].astype(jnp.float32)[gain : gain + 1]

        @pl.loop(0, 8)
        def _(p):
            here = pl.ds(pl.multiple_of(p * 32, 32), 32)
            v = resid[here, :]
            scale = lax.rsqrt(jnp.mean(v * v, axis=-1, keepdims=True) + EPS)
            lhs[dest, here, :] = (v * scale * gains).astype(jnp.bfloat16)

    def granule(kind, l, u, pair, half, j):
        product(l, u, pair)
        lanes = pl.ds(pl.multiple_of(half * 256, 256), 256)

        @pl.when(kind == 0)
        def _():
            @pl.loop(0, 4)
            def _(p):
                here = pl.ds(pl.multiple_of(p * 64, 64), 64)
                resid[here, lanes] += acc[here, :]

        @pl.when(kind == 1)
        def _():
            @pl.loop(0, 4)
            def _(p):
                here = pl.ds(pl.multiple_of(p * 64, 64), 64)
                lhs[5, here, lanes] = jax.nn.gelu(acc[here, :]).astype(jnp.bfloat16)

        @pl.when(kind == 2)
        def _():
            first = pl.ds(pl.multiple_of(half * 256, 128), 128)
            second = pl.ds(pl.multiple_of(jnp.minimum(half * 256 + 128, 1536), 128), 128)

            @pl.loop(0, 4)
            def _(p):
                here = pl.ds(pl.multiple_of(p * 64, 64), 64)
                t = acc[here, :].astype(jnp.bfloat16).astype(jnp.float32)
                t0 = t[:, :128]
                t1 = jnp.where(half < 6, t[:, 128:], LOW)
                rows = pl.ds(pl.multiple_of(peer(j) * 256 + p * 64, 64), 64)
                s0 = sv[rows, first].astype(jnp.float32)
                s1 = sv[rows, second].astype(jnp.float32)
                old = tops[0, rows, :]
                new = jnp.maximum(old, jnp.maximum(t0, t1))
                fade = jnp.exp(old - new)
                e0, e1 = jnp.exp(t0 - new), jnp.exp(t1 - new)
                tops[0, rows, :] = new
                sums[0, rows, :] = sums[0, rows, :] * fade + (e0 + e1)
                tcr[rows, :] = tcr[rows, :] * fade + (e0 * (t0 - s0) + e1 * (t1 - s1))

    def ready(n):
        n = jnp.clip((TREES * (n + 1) - 40) // 4, 0, 7)
        return n

    def share(i, l, dest, j):
        return pltpu.make_async_remote_copy(
            lhs.at[l], lhs.at[dest], fin_sent.at[i], fin_recv.at[i],
            device_id=(g, peer(j)), device_id_type=MESH,
        )

    @pl.loop(0, SLOTS + 8)
    def _(s):
        forward(s)
        n = s - BASE

        @pl.when(s == STUDENT)
        def _():
            load_feat.wait()
            load_stud.wait()

        @pl.when((s >= STUDENT) & (s < STUDENT + 16))
        def _():
            student_stats(s - STUDENT)

        student = (s >= STUDENT + 16) & (s < STUDENT + 24)
        late = s >= SLOTS
        @pl.when(student | late)
        def _():
            gather_stats(jnp.where(late, 0, 1), jnp.where(late, s - SLOTS, s - STUDENT - 16))

        @pl.when((n > PAIR0) & (n <= PAIR1))
        def _():
            @pl.loop(0, TREES)
            def _(t):
                block = w.at[BASE_B + t * PAIR1 + n - 1]
                pltpu.make_async_copy(block, block, pair_recv.at[t, n - 1]).wait()

        @pl.when(n == 0)
        def _():
            convolve()

        def made(n):
            total = jnp.int32(0)
            for step, upto in ((2, 1), (3, 3), (4, 6), (5, 9), (6, 10), (7, 14), (8, 16)):
                total = jnp.where(n >= step, upto, total)
            return total

        first = n == 1
        done = made(n - 1)
        count = jnp.where(first, 2, made(n) - done)

        def due(i):
            made_now = done + i
            part = made_now % 4
            kind = jnp.where(first | (part >= 2), 0, 1)
            l = jnp.where(first | (part < 2), 4, 5)
            u = jnp.where(first, 4 * i, 8 + 16 * (made_now // 8) + 4 * part)
            pair = jnp.where(first, 0, (made_now // 4) % 2)
            half = jnp.where(first, i, part % 2)
            return kind, l, u, pair, half

        starts = (9, 10, 12, 13)
        los, his = [], []
        for j in range(4):
            los.append(jnp.where(n - 1 >= starts[j], ready(n - 1), 0))
            his.append(jnp.where(n >= starts[j], ready(n), 0))

        @pl.when(n == 10)
        def _():
            share(0, 1, 1, 1).wait_recv()

        @pl.when(n == 12)
        def _():
            share(1, 2, 2, 2).wait_recv()
            share(2, 2, 3, 1).start()

        @pl.when(n == 13)
        def _():
            share(2, 3, 3, 1).wait_recv()

        sizes = [his[j] - los[j] for j in range(4)]
        ends = [sizes[0], sizes[0] + sizes[1], sizes[0] + sizes[1] + sizes[2]]
        total = ends[2] + sizes[3]

        def step(i, _):
            q = i - count
            j = jnp.where(q < ends[0], 0, jnp.where(q < ends[1], 1, jnp.where(q < ends[2], 2, 3)))
            start = jnp.where(
                q < ends[0], los[0],
                jnp.where(q < ends[1], los[1] - ends[0], jnp.where(q < ends[2], los[2] - ends[1], los[3] - ends[2])),
            )
            slab = q + start
            cls = i >= count
            kind, l, u, pair, half = due(jnp.minimum(i, 3))
            granule(
                jnp.where(cls, 2, kind), jnp.where(cls, j, l), jnp.where(cls, 40 + 4 * slab, u),
                jnp.where(cls, 0, pair), jnp.where(cls, slab, half), j,
            )
            return 0

        lax.fori_loop(0, count + total, step, 0)

        @pl.when(n == 1)
        def _():
            normalize(4, 0)

        @pl.when(n == 8)
        def _():
            normalize(0, 1)
            share(0, 0, 1, 1).start()
            share(1, 0, 2, 2).start()

    for i, (l, dest, j) in enumerate(((0, 1, 1), (0, 2, 2), (2, 3, 1))):
        share(i, l, dest, j).wait_send()

    @pl.loop(0, TREES)
    def _(t):
        @pl.loop(0, role[8 + t])
        def _(d):
            part = w.at[pl.ds(t * STEPS, STEPS)]
            pltpu.make_async_copy(part, part, sent.at[t, d]).wait()

        part = w.at[pl.ds(BASE_B + t * PAIR1 + PAIR0, PAIR1 - PAIR0)]
        pltpu.make_async_copy(part, part, pair_sent.at[t]).wait()

    @pl.loop(0, role[8])
    def _(d):
        for i, ref in enumerate((ck, ng)):
            pltpu.make_async_copy(ref, ref, par_sent.at[i, d]).wait()

    for j in range(1, 4):
        tell(j).wait()
    rcv[0] = stat[c]
    got = [jnp.concatenate([rcv[j, 0, 0:3], rcv[j, 1, 0:2]], axis=0) for j in range(4)]
    tm = functools.reduce(jnp.maximum, [r[0:1] for r in got])
    sm = functools.reduce(jnp.maximum, [r[3:4] for r in got])
    tw = [jnp.exp(r[0:1] - tm) for r in got]
    ts = sum(r[1:2] * f for r, f in zip(got, tw))
    tc = sum(r[2:3] * f for r, f in zip(got, tw))
    ss = sum(r[4:5] * jnp.exp(r[3:4] - sm) for r in got)
    value = tc / ts - (tm + jnp.log(ts)) + (sm + jnp.log(ss))
    lane = lax.broadcasted_iota(jnp.int32, (1, 256), 1)
    out[...] = jnp.where(lane < lens[0], value, 0.0)


def call(root, *operands):
    hbm = pl.BlockSpec(memory_space=pl.ANY)
    f32, bf16 = jnp.float32, jnp.bfloat16
    return pl.pallas_call(
        functools.partial(kernel, root),
        out_shape=jax.ShapeDtypeStruct((1, 256), f32),
        in_specs=[pl.BlockSpec(memory_space=pltpu.SMEM)] + [hbm] * 8,
        out_specs=pl.BlockSpec(memory_space=pltpu.VMEM),
        scratch_shapes=[
            pltpu.VMEM((BASE_B + TREES * PAIR1, 256, 128), bf16),
            pltpu.VMEM((1024, 1664), bf16),
            pltpu.VMEM((256, 512), bf16),
            pltpu.VMEM((6, 256, 512), bf16),
            pltpu.VMEM((256, 512), f32),
            pltpu.VMEM((256, 256), f32),
            pltpu.VMEM((2, 1024, 128), f32),
            pltpu.VMEM((2, 1024, 128), f32),
            pltpu.VMEM((1024, 128), f32),
            pltpu.VMEM((4, 2, 8, 256), f32),
            pltpu.VMEM((4, 2, 8, 256), f32),
            pltpu.VMEM((1, 3, 512), bf16),
            pltpu.VMEM((1, 2, 512), bf16),
            pltpu.SMEM((48,), jnp.int32),
        ],
        compiler_params=pltpu.CompilerParams(collective_id=root, has_side_effects=True),
        name=f"teach{root}",
    )(*operands)


def body(features, student, lengths, source, pw, up, dn, cl, ck, ng):
    branches = [functools.partial(call, root) for root in range(pw_groups)]
    result = lax.switch(source[0], branches, lengths, features, student, pw, up, dn, cl, ck, ng)
    return result.reshape(256)


pw_groups = 32


def solution(mesh):
    return jax.shard_map(
        body,
        mesh=mesh,
        in_specs=(
            P(("group", "cls"), None),
            P("group", "cls"),
            P(("group", "cls")),
            P(),
            P("group", None, None),
            P("group", None, None),
            P("group", None, None),
            P("group", None, "cls"),
            P("group", None, None),
            P("group", None, None),
        ),
        out_specs=P(("group", "cls")),
        check_vma=False,
    )
```
